32 devices in a mesh: seq: 8 (over z, y), mp: 4 (over x, core).
Axes of the slice: x: 2, y: 2, z: 4, core: 2. Of those that a mesh axis runs over, the one named last changes fastest.
Arguments:
- tokens: bfloat16 [3072, 2048], P('seq'), may hold values from -24 to 24
- database: bfloat16 [64, 96, 896], P('seq'), may hold values from -24 to 24
- nb_shard: int32 [48, 2], replicated, may hold values from 0 to 7, all different within a row; in each aligned block of 6 rows (0 to 5, 6 to 11, ...) at most 2 rows name the same one
- nb_row: int32 [48, 2], replicated, may hold values from 0 to 7
- dec_gain: float32 [2048], replicated, may hold values from 0.1 to 1.9
- enc_gain: float32 [896], replicated, may hold values from 0.1 to 1.9
- w_in: bfloat16 [896, 1792], replicated, may hold values from -0.1875 to 0.1875
- w_out: bfloat16 [1792, 896], replicated, may hold values from -0.125 to 0.125
- w_query: bfloat16 [2048, 2048], P(None, 'mp'), may hold values from -0.125 to 0.125
- w_key: bfloat16 [896, 2048], P(None, 'mp'), may hold values from -0.1875 to 0.1875
- w_value: bfloat16 [896, 2048], P(None, 'mp'), may hold values from -0.1875 to 0.1875
- w_proj: bfloat16 [2048, 2048], P('mp'), may hold values from -0.5 to 0.5
- grad_out: bfloat16 [3072, 2048], P('seq'), may hold values from -6 to 6
Outputs:
- cca: bfloat16 [3072, 2048], P('seq', 'mp')
- grad_tokens: float32 [3072, 2048], P('seq', 'mp')
- grad_database: float32 [64, 96, 896], P('seq', 'mp')
The draws below stay inside these ranges and needn't reach their ends.
Inputs may be any that keep to these rules, and one draw needn't show every extreme that they name: `nb_shard`: in each aligned block of 6 stretches (the stretches of one device) no shard is named more than 2 times, and some block reaches it; the 2 neighbours of a stretch come from different shards.
All inputs are finite; a program needn't handle non-finite values.
Results may differ from the reference program's by a relative error of at most 0.017.
Values may be sent and summed in bfloat16 or wider, within the bound.
No kernel may reach another device: no remote copies, remote signals or barrier semaphores. Data moves between devices by JAX's collectives and lax.ppermute only.
A program may use at most 128 MiB of HBM per device.

```python
import math
import jax
import jax.numpy as jnp
import numpy as np
from jax import lax

D = 2048
HEADS = 16
HD = 128
E = 896
F = 1792
L = 96
STRETCH = 64
K = 2
SEQ_LEN = 4096
ROWS_DEV = 8
CH_DEV = 6
CAP = 2
TOKENS = 3072
STRETCHES = 48
DBROWS = 64
N_SEQ = 8


def scale_field(key, base, row_shape, col_shape):
    key_row, key_col = jax.random.split(jax.random.fold_in(key, 17))
    col_scale = jnp.exp(jax.random.uniform(key_col, col_shape, minval=math.log(0.2), maxval=math.log(2.0)))
    row_scale = jnp.exp(jax.random.uniform(key_row, row_shape, minval=math.log(0.3), maxval=math.log(3.0)))
    return (base * col_scale * row_scale).astype(jnp.bfloat16)


def draw_tokens(key, part):
    key_base = jax.random.fold_in(key, 0)
    base = jnp.clip(jax.random.normal(key_base, (TOKENS, D)), -4.0, 4.0)
    return scale_field(key, base, (TOKENS, 1), (1, D))


def draw_database(key, part):
    key_base = jax.random.fold_in(key, 0)
    base = jnp.clip(jax.random.normal(key_base, (DBROWS, L, E)), -4.0, 4.0)
    return scale_field(key, base, (DBROWS, L, 1), (1, 1, E))


def with_ends(result, key, least, largest):
    spot = [jax.random.randint(jax.random.fold_in(key, axis), (), 0, length) for axis, length in enumerate(result.shape)]
    widest = result.shape.index(max(result.shape))
    next_to = spot[:widest] + [(spot[widest] + 1) % result.shape[widest]] + spot[widest + 1:]
    return result.at[tuple(spot)].set(least).at[tuple(next_to)].set(largest)


def levels(stream_key, extent, cuts, low, top_value):
    level = 1.0
    for position, parts in cuts:
        steps = jax.random.uniform(jax.random.fold_in(jax.random.fold_in(stream_key, 6), position), (parts,), jnp.float32, low / len(cuts), top_value / len(cuts))
        level = level * jnp.repeat(jnp.exp(steps), extent[position] // parts).reshape((-1,) + (1,) * (len(extent) - 1 - position))
    return level


def assign_block(own_key, own, number, rows, amount, top, most, skew):
    ranking = jax.random.permutation(own_key, amount)
    packed, usual = load_shares(amount, rows * top, most, skew, True), load_shares(amount, rows * top, most, skew, False)
    places = jnp.arange(amount)

    def named(tallies, turn):
        used = int((tallies > 0).sum())
        fixed = max(1, used // 4)
        passed = fixed + (places - fixed + turn * (used - fixed)) % max(1, amount - fixed)
        return jnp.zeros((amount,), jnp.int32).at[ranking[jnp.where(places < fixed, places, passed)]].set(jnp.asarray(tallies, jnp.int32))

    tallies = jnp.where(number % 4 == 0, named(packed, number // 4), named(usual, number - number // 4 - 1))
    mixed = jax.random.permutation(jax.random.fold_in(own, 3), amount)
    source_of, receiver = mixed[0:amount // 2 * 2:2], mixed[1:amount // 2 * 2:2]
    margin = jnp.minimum(tallies[source_of] - 1, most - tallies[receiver]) // 2
    margin = jnp.where((source_of == ranking[0]) | (receiver == ranking[0]) | (tallies[receiver] == 0), 0, jnp.maximum(margin, 0))
    passed = jax.random.randint(jax.random.fold_in(own, 4), (amount // 2,), 0, 1 << 20) % (margin + 1)
    tallies = tallies.at[source_of].add(-passed).at[receiver].add(passed)
    items = jnp.searchsorted(jnp.cumsum(tallies), jnp.arange(rows * top), side="right").astype(jnp.int32)
    listing = items.reshape(top, rows).T
    listing = listing[jax.random.permutation(jax.random.fold_in(own, 1), rows)]
    turn = jax.random.randint(jax.random.fold_in(own, 2), (rows, 1), 0, top)
    return jnp.take_along_axis(listing, (jnp.arange(top)[None, :] + turn) % top, axis=1)


def load_shares(number_of, total, bound, lean, full):
    portions = [(1 << 20) // math.isqrt(rank ** lean) + 1 for rank in range(1, number_of + 1)]
    largest = bound if full else min(bound, max(-(-total // number_of), total * portions[0] // sum(portions)))
    least = 1 if total - largest >= number_of - 1 else 0
    given, spare = [largest] + [least] * (number_of - 1), total - largest - least * (number_of - 1)
    while spare > 0:
        free = [i for i in range(1, number_of) if given[i] < largest] or [i for i in range(1, number_of) if given[i] < bound]
        pool, remaining = sum([portions[i] for i in free]), spare
        for i in free:
            extra = min(bound - given[i], max(1, remaining * portions[i] // pool), spare)
            given[i] = given[i] + extra
            spare = spare - extra
    return np.array(given)


def scatter_about(stream_key, shape, deviation, limit, cuts=(), dtype=jnp.bfloat16):
    loudness = levels(stream_key, shape, cuts, -0.22, 0.18) if cuts else 1.0
    entries = jax.random.normal(stream_key, shape, jnp.float32) * deviation * loudness
    return jnp.minimum(jnp.maximum(entries, -limit), limit).astype(dtype)


def setup_inputs(seed: int = 0) -> dict:
    arg_keys = jax.random.split(jax.random.key(seed), 14)
    tokens = draw_tokens(jax.random.fold_in(arg_keys[13], 71), 0)
    database = draw_database(jax.random.fold_in(arg_keys[13], 71), 0)
    nb_shard_keys = jax.random.split(jax.random.fold_in(arg_keys[2], 1), STRETCHES // CH_DEV)
    nb_shard_turns = jax.random.permutation(jax.random.fold_in(arg_keys[2], 3), STRETCHES // CH_DEV)
    nb_shard = jax.vmap(lambda own, number: assign_block(jax.random.fold_in(arg_keys[2], 2), own, number, CH_DEV, N_SEQ, K, CAP, 2))(nb_shard_keys, nb_shard_turns).reshape((STRETCHES, K))
    nb_row = with_ends(jax.random.randint(arg_keys[3], (STRETCHES, K), 0, ROWS_DEV), jax.random.fold_in(arg_keys[3], 1), 0, ROWS_DEV - 1).astype(jnp.int32)
    dec_gain = jnp.clip(1.0 + 0.18 * jax.random.normal(arg_keys[4], (D,), jnp.float32), 0.1, 1.9)
    enc_gain = jnp.clip(1.0 + 0.18 * jax.random.normal(arg_keys[5], (E,), jnp.float32), 0.1, 1.9)
    w_in = scatter_about(arg_keys[6], (E, F), E ** -0.5, 0.1875)
    w_out = scatter_about(arg_keys[7], (F, E), F ** -0.5, 0.125)
    w_query = scatter_about(arg_keys[8], (D, D), D ** -0.5, 0.125, ((1, 4),))
    w_key = scatter_about(arg_keys[9], (E, D), E ** -0.5, 0.1875, ((1, 4),))
    w_value = scatter_about(arg_keys[10], (E, D), E ** -0.5, 0.1875, ((1, 4),))
    w_proj = scatter_about(arg_keys[11], (D, D), HD ** -0.5, 0.5, ((0, 4),))
    grad_out = scatter_about(arg_keys[12], (TOKENS, D), 1.0, 6.0, ((0, 8),))
    return {"tokens": tokens, "database": database, "nb_shard": nb_shard, "nb_row": nb_row, "dec_gain": dec_gain, "enc_gain": enc_gain, "w_in": w_in, "w_out": w_out, "w_query": w_query, "w_key": w_key, "w_value": w_value, "w_proj": w_proj, "grad_out": grad_out}


EPSILON = 1e-06

def rms_scaling(values):
    return lax.rsqrt(lax.optimization_barrier(jnp.mean(values * values, axis=-1, keepdims=True)) + EPSILON)

def silu_slope(pre_act):
    sigmoid = jax.nn.sigmoid(pre_act)
    return sigmoid * (1.0 + pre_act * (1.0 - sigmoid))

def dot_t(matrix, weight):
    return lax.dot_general(matrix, weight, (((1,), (1,)), ((), ())), preferred_element_type=jnp.float32)

def reference(tokens, database, nb_shard, nb_row, dec_gain, enc_gain, w_in, w_out, w_query, w_key, w_value, w_proj, grad_out):
    flat_rows = (nb_shard * ROWS_DEV + nb_row).reshape(-1).astype(jnp.int32)
    embedded = jnp.take(database, flat_rows, axis=0).reshape(-1, E)
    values = embedded.astype(jnp.float32)
    scaling = rms_scaling(values)
    unit_rows = values * scaling
    enc_scale = enc_gain.astype(jnp.float32)
    normed = (unit_rows * enc_scale).astype(jnp.bfloat16)
    pre_act = jnp.dot(normed, w_in, preferred_element_type=jnp.float32)
    hidden = jax.nn.silu(pre_act).astype(jnp.bfloat16)
    encoded = (values + jnp.dot(hidden, w_out, preferred_element_type=jnp.float32)).astype(jnp.bfloat16)
    key_rows = jnp.dot(encoded, w_key, preferred_element_type=jnp.float32).astype(jnp.bfloat16)
    value_rows = jnp.dot(encoded, w_value, preferred_element_type=jnp.float32).astype(jnp.bfloat16)
    tok_vals = tokens.astype(jnp.float32)
    tok_scaling = rms_scaling(tok_vals)
    tok_unit = tok_vals * tok_scaling
    dec_scale = dec_gain.astype(jnp.float32)
    tok_normed = (tok_unit * dec_scale).astype(jnp.bfloat16)
    query_rows = jnp.dot(tok_normed, w_query, preferred_element_type=jnp.float32).astype(jnp.bfloat16)
    query_blk = query_rows.reshape(STRETCHES, STRETCH, HEADS, HD).astype(jnp.float32)
    key_blk = key_rows.reshape(STRETCHES, K * L, HEADS, HD).astype(jnp.float32)
    value_blk = value_rows.reshape(STRETCHES, K * L, HEADS, HD).astype(jnp.float32)
    factor = HD ** (-0.5)
    scores = jnp.einsum('cqhd,ckhd->chqk', query_blk, key_blk) * factor
    exp_score = jnp.exp(scores)
    attn_prob = exp_score / lax.optimization_barrier(jnp.sum(exp_score, axis=-1, keepdims=True))
    attn_weight = attn_prob.astype(jnp.bfloat16).astype(jnp.float32)
    context = jnp.einsum('chqk,ckhd->cqhd', attn_weight, value_blk).astype(jnp.bfloat16).reshape(TOKENS, D)
    live_tok = (jnp.arange(TOKENS) // STRETCH % (SEQ_LEN // STRETCH) != 0)[:, None]
    cca = jnp.where(live_tok, jnp.dot(context, w_proj, preferred_element_type=jnp.float32), 0.0).astype(jnp.bfloat16)
    masked = jnp.where(live_tok, grad_out, jnp.zeros_like(grad_out))
    grad_ctx = dot_t(masked, w_proj).astype(jnp.bfloat16)
    grad_blk = grad_ctx.reshape(STRETCHES, STRETCH, HEADS, HD).astype(jnp.float32)
    grad_prob = jnp.einsum('cqhd,ckhd->chqk', grad_blk, value_blk)
    grad_score = (attn_prob * (grad_prob - lax.optimization_barrier(jnp.sum(attn_prob * grad_prob, axis=-1, keepdims=True))) * factor).astype(jnp.bfloat16).astype(jnp.float32)
    grad_value = jnp.einsum('chqk,cqhd->ckhd', attn_weight, grad_blk).astype(jnp.bfloat16).reshape(-1, D)
    grad_query = jnp.einsum('chqk,ckhd->cqhd', grad_score, key_blk).astype(jnp.bfloat16).reshape(TOKENS, D)
    grad_key = jnp.einsum('chqk,cqhd->ckhd', grad_score, query_blk).astype(jnp.bfloat16).reshape(-1, D)
    grad_normed = dot_t(grad_query, w_query)
    tok_grad = grad_normed * dec_scale
    grad_tokens = tok_scaling * (tok_grad - tok_unit * lax.optimization_barrier(jnp.mean(tok_grad * tok_unit, axis=-1, keepdims=True)))
    grad_enc = dot_t(grad_key, w_key) + dot_t(grad_value, w_value)
    grad_hidden = dot_t(grad_enc.astype(jnp.bfloat16), w_out)
    grad_pre = (grad_hidden * silu_slope(pre_act)).astype(jnp.bfloat16)
    grad_unit = dot_t(grad_pre, w_in) * enc_scale
    grad_embed = grad_enc + scaling * (grad_unit - unit_rows * lax.optimization_barrier(jnp.mean(grad_unit * unit_rows, axis=-1, keepdims=True)))
    grad_database = jnp.zeros((DBROWS, L, E), jnp.float32).at[flat_rows].add(grad_embed.reshape(-1, L, E))
    return (cca, grad_tokens, grad_database)
```

```python
import jax
import jax.numpy as jnp
from jax import lax
from jax.experimental import pallas as pl
from jax.experimental.pallas import tpu as pltpu
from jax.sharding import PartitionSpec as P

HD = 128
L = 96
STRETCH = 64
K = 2
SEQ_LEN = 4096


EPSILON = 1e-06


def rms_scaling(values):
    return lax.rsqrt(jnp.mean(values * values, axis=-1, keepdims=True) + EPSILON)


def silu_slope(pre_act):
    sigmoid = jax.nn.sigmoid(pre_act)
    return sigmoid * (1.0 + pre_act * (1.0 - sigmoid))


def dot_t(matrix, weight):
    return lax.dot_general(
        matrix, weight, (((1,), (1,)), ((), ())), preferred_element_type=jnp.float32
    )


def encode(embedded, enc_gain, w_in, w_out):
    values = embedded.astype(jnp.float32)
    scaling = rms_scaling(values)
    normed = (values * scaling * enc_gain).astype(jnp.bfloat16)
    pre_act = jnp.einsum("nle,ef->nlf", normed, w_in, preferred_element_type=jnp.float32)
    hidden = jax.nn.silu(pre_act).astype(jnp.bfloat16)
    mixed = jnp.einsum("nlf,fe->nle", hidden, w_out, preferred_element_type=jnp.float32)
    encoded = (values + mixed).astype(jnp.bfloat16)
    return (encoded, pre_act, scaling)


def encode_back(embedded, pre_act, scaling, grad_enc, enc_gain, w_in, w_out):
    grad_hidden = jnp.einsum(
        "nle,fe->nlf", grad_enc.astype(jnp.bfloat16), w_out, preferred_element_type=jnp.float32
    )
    grad_pre = (grad_hidden * silu_slope(pre_act)).astype(jnp.bfloat16)
    grad_unit = (
        jnp.einsum("nlf,ef->nle", grad_pre, w_in, preferred_element_type=jnp.float32) * enc_gain
    )
    unit_rows = embedded.astype(jnp.float32) * scaling
    return grad_enc + scaling * (
        grad_unit - unit_rows * jnp.mean(grad_unit * unit_rows, axis=-1, keepdims=True)
    )


def general_body(
    tokens,
    database,
    nb_shard,
    nb_row,
    dec_gain,
    enc_gain,
    w_in,
    w_out,
    w_query,
    w_key,
    w_value,
    w_proj,
    grad_out,
):
    seq_count = lax.axis_size("seq")
    my_seq = lax.axis_index("seq")
    mp_count = lax.axis_size("mp")
    my_mp = lax.axis_index("mp")
    tok_rows = tokens.shape[0]
    stretches_here = tok_rows // STRETCH
    width = w_query.shape[1]
    heads_here = width // HD
    nb_here = stretches_here * K
    slot_cap = max(1, (nb_here + seq_count - 1) // seq_count)
    slot_count = seq_count * slot_cap
    tok_span = database.shape[1] // mp_count
    tok_start = my_mp * tok_span
    requests = nb_shard.reshape(seq_count, nb_here)
    req_rows = nb_row.reshape(seq_count, nb_here)
    req_order = jnp.arange(nb_here)
    same_shard = requests[:, :, None] == requests[:, None, :]
    before = req_order[None, :] < req_order[:, None]
    slot_rank = jnp.sum((same_shard & before[None]).astype(jnp.int32), axis=2)
    held_here = requests == my_seq
    slot_ids = jnp.arange(slot_cap)
    slot_pick = held_here[:, None, :] & (slot_rank[:, None, :] == slot_ids[None, :, None])
    slot_row = jnp.sum(slot_pick.astype(jnp.int32) * req_rows[:, None, :], axis=2).reshape(
        slot_count
    )
    slot_live = jnp.any(slot_pick, axis=2).reshape(slot_count)
    own_req = lax.dynamic_index_in_dim(requests, my_seq, 0, keepdims=False)
    own_rank = lax.dynamic_index_in_dim(slot_rank, my_seq, 0, keepdims=False)
    source = own_req * slot_cap + own_rank
    kv_weight = jnp.concatenate([w_key, w_value], axis=1)
    own_slice = lax.dynamic_slice_in_dim(database, tok_start, tok_span, 1)
    outgoing = jnp.take(own_slice, slot_row, axis=0)
    arrived = lax.all_to_all(outgoing, "seq", split_axis=0, concat_axis=0, tiled=True)
    embed_part = jnp.take(arrived, source, axis=0)
    enc_part, pre_part, scale_part = encode(embed_part, enc_gain, w_in, w_out)
    kv_rows = jnp.einsum(
        "nle,ef->nlf",
        lax.all_gather(enc_part, "mp", axis=1, tiled=True),
        kv_weight,
        preferred_element_type=jnp.float32,
    ).astype(jnp.bfloat16)
    key_rows = kv_rows[:, :, :width]
    value_rows = kv_rows[:, :, width:]
    tok_vals = tokens.astype(jnp.float32)
    tok_scaling = rms_scaling(tok_vals)
    tok_unit = tok_vals * tok_scaling
    tok_normed = (tok_unit * dec_gain).astype(jnp.bfloat16)
    query_rows = jnp.dot(tok_normed, w_query, preferred_element_type=jnp.float32).astype(
        jnp.bfloat16
    )
    query_blk = query_rows.reshape(stretches_here, STRETCH, heads_here, HD)
    key_blk = key_rows.reshape(stretches_here, K * L, heads_here, HD)
    value_blk = value_rows.reshape(stretches_here, K * L, heads_here, HD)
    factor = HD ** (-0.5)
    scores = (
        jnp.einsum("cqhd,ckhd->chqk", query_blk, key_blk, preferred_element_type=jnp.float32)
        * factor
    )
    exp_score = jnp.exp(scores)
    attn_prob = exp_score / jnp.sum(exp_score, axis=-1, keepdims=True)
    attn_weight = attn_prob.astype(jnp.bfloat16)
    context = (
        jnp.einsum("chqk,ckhd->cqhd", attn_weight, value_blk, preferred_element_type=jnp.float32)
        .astype(jnp.bfloat16)
        .reshape(tok_rows, width)
    )
    stretch_pos = (my_seq * stretches_here + jnp.arange(stretches_here)) % (SEQ_LEN // STRETCH)
    live_tok = jnp.repeat(stretch_pos != 0, STRETCH)[:, None]
    out_terms = jnp.where(
        live_tok, jnp.dot(context, w_proj, preferred_element_type=jnp.float32), 0.0
    )
    masked = jnp.where(live_tok, grad_out, jnp.zeros_like(grad_out))
    grad_ctx = dot_t(masked, w_proj).astype(jnp.bfloat16)
    grad_blk = grad_ctx.reshape(stretches_here, STRETCH, heads_here, HD)
    grad_prob = jnp.einsum(
        "cqhd,ckhd->chqk", grad_blk, value_blk, preferred_element_type=jnp.float32
    )
    grad_score = (
        attn_prob * (grad_prob - jnp.sum(attn_prob * grad_prob, axis=-1, keepdims=True)) * factor
    ).astype(jnp.bfloat16)
    grad_value = jnp.einsum(
        "chqk,cqhd->ckhd", attn_weight, grad_blk, preferred_element_type=jnp.float32
    ).astype(jnp.bfloat16)
    grad_query = (
        jnp.einsum("chqk,ckhd->cqhd", grad_score, key_blk, preferred_element_type=jnp.float32)
        .astype(jnp.bfloat16)
        .reshape(tok_rows, width)
    )
    grad_key = jnp.einsum(
        "chqk,cqhd->ckhd", grad_score, query_blk, preferred_element_type=jnp.float32
    ).astype(jnp.bfloat16)
    key_grad = grad_key.reshape(nb_here, L, width)
    value_grad = grad_value.reshape(nb_here, L, width)
    enc_terms = jnp.einsum("nlf,ef->nle", key_grad, w_key, preferred_element_type=jnp.float32)
    enc_terms = enc_terms + jnp.einsum(
        "nlf,ef->nle", value_grad, w_value, preferred_element_type=jnp.float32
    )
    grad_enc = lax.psum_scatter(
        enc_terms.astype(jnp.bfloat16), "mp", scatter_dimension=1, tiled=True
    ).astype(jnp.float32)
    grad_normed = dot_t(grad_query, w_query)
    tok_grad = grad_normed * dec_gain
    tok_terms = tok_scaling * (
        tok_grad - tok_unit * jnp.mean(tok_grad * tok_unit, axis=-1, keepdims=True)
    )
    grad_embed = encode_back(embed_part, pre_part, scale_part, grad_enc, enc_gain, w_in, w_out)
    place_back = (source[:, None] == jnp.arange(slot_count)[None, :]).astype(jnp.float32)
    returned = jnp.einsum("ns,nle->sle", place_back, grad_embed, precision=lax.Precision.HIGHEST)
    received = lax.all_to_all(
        returned.astype(jnp.bfloat16), "seq", split_axis=0, concat_axis=0, tiled=True
    ).astype(returned.dtype)
    row_hit = (
        (slot_row[None, :] == jnp.arange(database.shape[0])[:, None]) & slot_live[None, :]
    ).astype(jnp.float32)
    grad_database = jnp.einsum("rs,sle->rle", row_hit, received, precision=lax.Precision.HIGHEST)
    cca_sum, grad_sum = (
        lax.psum_scatter(
            out_terms.astype(jnp.bfloat16), "mp", scatter_dimension=1, tiled=True
        ).astype(jnp.float32),
        lax.psum_scatter(
            tok_terms.astype(jnp.bfloat16), "mp", scatter_dimension=1, tiled=True
        ).astype(jnp.float32),
    )
    return (cca_sum.astype(jnp.bfloat16), grad_sum, grad_database)


BF16 = jnp.bfloat16
F32 = jnp.float32

VMEM_SPEC = pl.BlockSpec(memory_space=pltpu.VMEM)
SMEM_SPEC = pl.BlockSpec(memory_space=pltpu.SMEM)
ANY_SPEC = pl.BlockSpec(memory_space=pl.ANY)


def fast_ok(mesh):
    return mesh.shape["mp"] == 4 and mesh.shape["seq"] == 8


def cost(flops, nbytes):
    return pl.CostEstimate(flops=flops, bytes_accessed=nbytes, transcendentals=0)


def dot_nn(a, b):
    return lax.dot_general(a, b, (((1,), (0,)), ((), ())), preferred_element_type=F32)


def dot_nt(a, b):
    return lax.dot_general(a, b, (((1,), (1,)), ((), ())), preferred_element_type=F32)


def dot_tn(a, b):
    return lax.dot_general(a, b, (((0,), (0,)), ((), ())), preferred_element_type=F32)


def requested(shard_ref, row_ref, owner, shard, count, cap):
    rows = [jnp.int32(0)] * cap
    places = [jnp.int32(0)] * cap
    seen = jnp.int32(0)
    for i in range(count):
        c, j = owner * (count // K) + i // K, i % K
        hit = shard_ref[j, c] == shard
        row = row_ref[j, c]
        for s in range(cap):
            take = hit & (seen == s)
            rows[s] = jnp.where(take, row, rows[s])
            places[s] = jnp.where(take, i, places[s])
        seen = seen + hit.astype(jnp.int32)
    return rows, places, seen


def encode_kernel(dims, shard_ref, row_ref, gain_ref, db_ref, w_in_ref, w_out_ref, *rest):
    n_seq, cap, nb_here, rows, span, width, hidden_n, tile = dims
    chunks = rest[:n_seq]
    pre_ref, db_buf, w1_buf, w2_buf, acc, enc_buf, db_sem, w_sem = rest[n_seq:]
    me, my_mp = lax.axis_index("seq"), lax.axis_index("mp")
    db_copy = pltpu.make_async_copy(db_ref.at[:, my_mp], db_buf, db_sem)
    db_copy.start()
    steps = hidden_n // tile
    copies = []
    for f in range(steps):
        one = pltpu.make_async_copy(
            w_in_ref.at[:, pl.ds(f * tile, tile)], w1_buf.at[f], w_sem.at[f, 0]
        )
        two = pltpu.make_async_copy(
            w_out_ref.at[pl.ds(f * tile, tile), :], w2_buf.at[f], w_sem.at[f, 1]
        )
        one.start()
        two.start()
        copies.append((one, two))
    picks = [
        requested(shard_ref, row_ref, jnp.bitwise_xor(me, k), me, nb_here, cap)[0]
        for k in range(n_seq)
    ]
    db_copy.wait()
    values = db_buf[...].astype(F32).reshape(rows * span, width)
    scaling = lax.rsqrt(jnp.mean(values * values, axis=-1, keepdims=True) + EPSILON)
    normed = (values * scaling * gain_ref[...]).astype(BF16)
    acc[...] = values
    for f in range(steps):
        copies[f][0].wait()
        pre = dot_nn(normed, w1_buf[f])
        pre_ref[:, f * tile : (f + 1) * tile] = pre
        hid = (pre * jax.nn.sigmoid(pre)).astype(BF16)
        copies[f][1].wait()
        acc[...] += dot_nn(hid, w2_buf[f])
    enc_buf[...] = acc[...].reshape(rows, span, width)
    for k in range(n_seq):
        for s in range(cap):
            chunks[k][s] = enc_buf[picks[k][s]].astype(BF16)


def encode_call(dims, shard_t, row_t, gain, db4, w_in, w_out):
    n_seq, cap, nb_here, rows, span, width, hidden_n, tile = dims
    steps = hidden_n // tile
    return pl.pallas_call(
        lambda *refs: encode_kernel(dims, *refs),
        out_shape=[jax.ShapeDtypeStruct((cap, span, width), BF16)] * n_seq
        + [jax.ShapeDtypeStruct((rows * span, hidden_n), F32)],
        in_specs=[SMEM_SPEC, SMEM_SPEC, VMEM_SPEC, ANY_SPEC, ANY_SPEC, ANY_SPEC],
        out_specs=[VMEM_SPEC] * (n_seq + 1),
        scratch_shapes=[
            pltpu.VMEM((rows, span, width), BF16),
            pltpu.VMEM((steps, width, tile), BF16),
            pltpu.VMEM((steps, tile, width), BF16),
            pltpu.VMEM((rows * span, width), F32),
            pltpu.VMEM((rows, span, width), F32),
            pltpu.SemaphoreType.DMA,
            pltpu.SemaphoreType.DMA((steps, 2)),
        ],
        cost_estimate=cost(4 * rows * span * width * hidden_n, 4 * width * hidden_n),
        name="encode",
    )(shard_t, row_t, gain, db4, w_in, w_out)


def pack_kernel(dims, shard_ref, row_ref, *rest):
    n_seq, cap, nb_here = dims
    own, across = rest[:n_seq], rest[n_seq : 2 * n_seq]
    out_ref, sem = rest[2 * n_seq :]
    me = lax.axis_index("seq")
    waits = []
    for k in range(n_seq):
        _, places, seen = requested(
            shard_ref, row_ref, me, jnp.bitwise_xor(me, k), nb_here, cap
        )
        for s in range(cap):
            copies = [
                pltpu.make_async_copy(
                    src.at[s], out_ref.at[b, places[s]], sem.at[k * cap + s, b]
                )
                for b, src in enumerate((own[k], across[k]))
            ]
            waits.append((seen > s, copies))

            @pl.when(seen > s)
            def _():
                for copy in copies:
                    copy.start()

    for live, copies in waits:

        @pl.when(live)
        def _():
            for copy in copies:
                copy.wait()


def pack_call(dims, shard_t, row_t, own, across):
    n_seq, cap, nb_here = dims
    _, span, width = own[0].shape
    return pl.pallas_call(
        lambda *refs: pack_kernel(dims, *refs),
        out_shape=jax.ShapeDtypeStruct((2, nb_here, span, width), BF16),
        in_specs=[SMEM_SPEC] * 2 + [ANY_SPEC] * (2 * n_seq),
        out_specs=VMEM_SPEC,
        scratch_shapes=[pltpu.SemaphoreType.DMA((n_seq * cap, 2))],
        cost_estimate=cost(0, 4 * nb_here * span * width * 2),
        name="pack",
    )(shard_t, row_t, *own, *across)


def query_kernel(tok_ref, gain_ref, w_ref, out_ref):
    values = tok_ref[...].astype(F32)
    scaling = lax.rsqrt(jnp.mean(values * values, axis=-1, keepdims=True) + EPSILON)
    normed = (values * scaling * gain_ref[...]).astype(BF16)
    out_ref[...] = dot_nn(normed, w_ref[...]).astype(BF16)


def query_call(tokens, gain, w_query, block):
    rows, width = tokens.shape
    cols = w_query.shape[1]
    return pl.pallas_call(
        query_kernel,
        out_shape=jax.ShapeDtypeStruct((rows, cols), BF16),
        grid=(rows // block,),
        in_specs=[
            pl.BlockSpec((block, width), lambda i: (i, 0)),
            pl.BlockSpec((1, width), lambda i: (0, 0)),
            pl.BlockSpec((width, cols), lambda i: (0, 0)),
        ],
        out_specs=pl.BlockSpec((block, cols), lambda i: (i, 0)),
        cost_estimate=cost(2 * rows * width * cols, 2 * width * (rows + cols)),
        name="query",
    )(tokens, gain, w_query)


def live_rows(block, tok_rows):
    first = lax.axis_index("seq") * tok_rows + pl.program_id(0) * block
    tok = first + lax.broadcasted_iota(jnp.int32, (block, 1), 0)
    return (tok // STRETCH) % (SEQ_LEN // STRETCH) != 0


def grad_ctx_kernel(tok_rows, grad_ref, w_ref, out_ref):
    live = live_rows(grad_ref.shape[0], tok_rows)
    grad = grad_ref[...].astype(F32)
    masked = jnp.where(live, grad, 0.0).astype(BF16)
    out_ref[...] = dot_nt(masked, w_ref[...]).astype(BF16)


def grad_ctx_call(grad_out, w_proj, block):
    rows, width = grad_out.shape
    cols = w_proj.shape[0]
    return pl.pallas_call(
        lambda *refs: grad_ctx_kernel(rows, *refs),
        out_shape=jax.ShapeDtypeStruct((rows, cols), BF16),
        grid=(rows // block,),
        in_specs=[
            pl.BlockSpec((block, width), lambda i: (i, 0)),
            pl.BlockSpec((cols, width), lambda i: (0, 0)),
        ],
        out_specs=pl.BlockSpec((block, cols), lambda i: (i, 0)),
        cost_estimate=cost(2 * rows * width * cols, 2 * width * (rows + cols)),
        name="grad_ctx",
    )(grad_out, w_proj)


def attend_kernel(
    mine_ref,
    part_ref,
    q_ref,
    g_ref,
    wk_ref,
    wv_ref,
    ctx_ref,
    gq_ref,
    keep_ref,
    send_ref,
    key_buf,
    value_buf,
    gk_buf,
    gv_buf,
):
    width = mine_ref.shape[-1]
    half = 2 * mine_ref.shape[1]
    encoded = jnp.concatenate(
        [mine_ref[...].reshape(half, width), part_ref[...].reshape(half, width)], axis=0
    )
    key_buf[...] = dot_nn(encoded, wk_ref[...]).astype(BF16)
    value_buf[...] = dot_nn(encoded, wv_ref[...]).astype(BF16)
    factor = HD ** (-0.5)
    for h in range(q_ref.shape[1] // HD):
        cols = slice(h * HD, (h + 1) * HD)
        query, key, value, grad = q_ref[:, cols], key_buf[:, cols], value_buf[:, cols], g_ref[:, cols]
        exp_score = jnp.exp(dot_nt(query, key) * factor)
        prob = exp_score / jnp.sum(exp_score, axis=-1, keepdims=True)
        weight = prob.astype(BF16)
        ctx_ref[:, cols] = dot_nn(weight, value).astype(BF16)
        grad_prob = dot_nt(grad, value)
        total = jnp.sum(prob * grad_prob, axis=-1, keepdims=True)
        grad_score = (prob * (grad_prob - total) * factor).astype(BF16)
        gq_ref[:, cols] = dot_nn(grad_score, key).astype(BF16)
        gv_buf[:, cols] = dot_tn(weight, grad).astype(BF16)
        gk_buf[:, cols] = dot_tn(grad_score, query).astype(BF16)
    terms = dot_nt(gk_buf[...], wk_ref[...]) + dot_nt(gv_buf[...], wv_ref[...])
    keep_ref[...] = terms[:half].astype(BF16).reshape(keep_ref.shape)
    send_ref[...] = terms[half:].astype(BF16).reshape(send_ref.shape)


def attend_call(first, count, mine, part, query, grad, w_key, w_value):
    _, rows, width = mine.shape
    cols = w_key.shape[1]
    stretches = query.shape[0] // STRETCH
    per = rows // stretches
    enc_spec = pl.BlockSpec((2, per, width), lambda i: (0, i + first, 0))
    tok_spec = pl.BlockSpec((STRETCH, cols), lambda i: (i + first, 0))
    w_spec = pl.BlockSpec((width, cols), lambda i: (0, 0))
    out_tok = pl.BlockSpec((STRETCH, cols), lambda i: (i, 0))
    out_enc = pl.BlockSpec((2, per, width), lambda i: (0, i, 0))
    keys = 4 * per
    return pl.pallas_call(
        attend_kernel,
        out_shape=[jax.ShapeDtypeStruct((count * STRETCH, cols), BF16)] * 2
        + [jax.ShapeDtypeStruct((2, count * per, width), BF16)] * 2,
        grid=(count,),
        in_specs=[enc_spec, enc_spec, tok_spec, tok_spec, w_spec, w_spec],
        out_specs=[out_tok, out_tok, out_enc, out_enc],
        scratch_shapes=[pltpu.VMEM((keys, cols), BF16)] * 4,
        cost_estimate=cost(
            count * (8 * keys * width * cols + 12 * STRETCH * keys * cols),
            4 * width * cols + count * 8 * keys * width,
        ),
        name="attend",
    )(mine, part, query, grad, w_key, w_value)


def project_kernel(tok_rows, ctx_ref, w_ref, keep_ref, send_ref):
    my_mp = lax.axis_index("mp")
    live = live_rows(ctx_ref.shape[0], tok_rows)
    part = keep_ref.shape[-1]
    context = ctx_ref[...]
    for j in range(4):
        start = pl.multiple_of(jnp.bitwise_xor(my_mp, j) * part, part)
        out = jnp.where(live, dot_nn(context, w_ref[:, pl.ds(start, part)]), 0.0)
        (keep_ref, send_ref)[j % 2][j // 2] = out.astype(BF16)


def pair_specs(block, part):
    return [pl.BlockSpec((2, block, part), lambda i: (0, i, 0))] * 2


def project_call(context, w_proj, block):
    rows, depth = context.shape
    width = w_proj.shape[1]
    part = width // 4
    return pl.pallas_call(
        lambda *refs: project_kernel(rows, *refs),
        out_shape=[jax.ShapeDtypeStruct((2, rows, part), BF16)] * 2,
        grid=(rows // block,),
        in_specs=[
            pl.BlockSpec((block, depth), lambda i: (i, 0)),
            pl.BlockSpec((depth, width), lambda i: (0, 0)),
        ],
        out_specs=pair_specs(block, part),
        cost_estimate=cost(2 * rows * depth * width, 2 * width * (rows + depth)),
        name="project",
    )(context, w_proj)


def tok_grad_kernel(tok_ref, gain_ref, gq_ref, w_ref, keep_ref, send_ref, unit_buf, grad_buf):
    my_mp = lax.axis_index("mp")
    part = keep_ref.shape[-1]
    values = tok_ref[...].astype(F32)
    scaling = lax.rsqrt(jnp.mean(values * values, axis=-1, keepdims=True) + EPSILON)
    unit = values * scaling
    grad = dot_nt(gq_ref[...], w_ref[...]) * gain_ref[...]
    mean = jnp.mean(grad * unit, axis=-1, keepdims=True)
    grad_buf[...] = scaling * (grad - unit * mean)
    for j in range(4):
        start = pl.multiple_of(jnp.bitwise_xor(my_mp, j) * part, part)
        (keep_ref, send_ref)[j % 2][j // 2] = grad_buf[:, pl.ds(start, part)].astype(BF16)


def tok_grad_call(tokens, gain, grad_query, w_query, block):
    rows, width = tokens.shape
    depth = grad_query.shape[1]
    part = width // 4
    return pl.pallas_call(
        tok_grad_kernel,
        out_shape=[jax.ShapeDtypeStruct((2, rows, part), BF16)] * 2,
        grid=(rows // block,),
        in_specs=[
            pl.BlockSpec((block, width), lambda i: (i, 0)),
            pl.BlockSpec((1, width), lambda i: (0, 0)),
            pl.BlockSpec((block, depth), lambda i: (i, 0)),
            pl.BlockSpec((width, depth), lambda i: (0, 0)),
        ],
        out_specs=pair_specs(block, part),
        scratch_shapes=[pltpu.VMEM((8, 128), F32), pltpu.VMEM((block, width), F32)],
        cost_estimate=cost(2 * rows * depth * width, 2 * width * (2 * rows + depth)),
        name="tok_grad",
    )(tokens, gain, grad_query, w_query)


def spread_kernel(dims, shard_ref, row_ref, *rest):
    n_seq, cap, nb_here, halves = dims
    terms, chunks, sums = rest[: 3 * halves], rest[3 * halves : -1], rest[-1]
    me = lax.axis_index("seq")
    per = nb_here // halves
    for p in range(halves):
        keep, recv, across = terms[3 * p : 3 * p + 3]
        sums[p * per : (p + 1) * per] = (
            keep[0].astype(F32) + recv[0].astype(F32) + across[...].astype(F32)
        )
    for k in range(n_seq):
        _, places, seen = requested(
            shard_ref, row_ref, me, jnp.bitwise_xor(me, k), nb_here, cap
        )
        for s in range(cap):
            chunks[k][s] = sums[places[s]].astype(BF16)


def spread_call(dims, shard_t, row_t, terms):
    n_seq, cap, nb_here, halves = dims
    _, per, span, width = terms[0].shape
    front = pl.BlockSpec((1, per, span, width), lambda i: (0, 0, 0, 0))
    whole = pl.BlockSpec((per, span, width), lambda i: (0, 0, 0))
    chunk = pl.BlockSpec((cap, span, width), lambda i: (0, 0, 0))
    return pl.pallas_call(
        lambda *refs: spread_kernel(dims, *refs),
        out_shape=[jax.ShapeDtypeStruct((cap, span, width), BF16)] * n_seq,
        grid=(1,),
        in_specs=[SMEM_SPEC] * 2 + [front, front, whole] * halves,
        out_specs=[chunk] * n_seq,
        scratch_shapes=[pltpu.VMEM((nb_here, span, width), F32)],
        cost_estimate=cost(0, 2 * 5 * nb_here * span * width),
        name="spread",
    )(shard_t, row_t, *terms)


def encode_back_kernel(
    dims, shard_ref, row_ref, gain_ref, db_ref, pre_ref, w_in_ref, w_out_ref, *rest
):
    n_seq, cap, nb_here, rows, span, width, hidden_n, tile = dims
    chunks = rest[:n_seq]
    out_ref, db_buf, pre_buf, w1_buf, w2_buf, total, acc, db_sem, pre_sem, w_sem = rest[n_seq:]
    me, my_mp = lax.axis_index("seq"), lax.axis_index("mp")
    db_copy = pltpu.make_async_copy(db_ref.at[:, my_mp], db_buf, db_sem)
    pre_copy = pltpu.make_async_copy(pre_ref, pre_buf, pre_sem)
    steps = hidden_n // tile
    copies = []
    for f in range(steps):
        one = pltpu.make_async_copy(
            w_in_ref.at[:, pl.ds(f * tile, tile)], w1_buf.at[f], w_sem.at[f, 0]
        )
        two = pltpu.make_async_copy(
            w_out_ref.at[pl.ds(f * tile, tile), :], w2_buf.at[f], w_sem.at[f, 1]
        )
        two.start()
        if f == 0:
            pre_copy.start()
        one.start()
        copies.append((one, two))
    db_copy.start()
    total[...] = jnp.zeros_like(total)
    for k in range(n_seq):
        picks, _, seen = requested(
            shard_ref, row_ref, jnp.bitwise_xor(me, k), me, nb_here, cap
        )
        for s in range(cap):

            @pl.when(seen > s)
            def _():
                total[picks[s]] += chunks[k][s].astype(F32)

    grad_enc = total[...].reshape(rows * span, width)
    grad_in = grad_enc.astype(BF16)
    pre_copy.wait()
    for f in range(steps):
        copies[f][1].wait()
        grad_hidden = dot_nt(grad_in, w2_buf[f])
        slope = silu_slope(pre_buf[:, f * tile : (f + 1) * tile])
        grad_pre = (grad_hidden * slope).astype(BF16)
        copies[f][0].wait()
        term = dot_nt(grad_pre, w1_buf[f])
        if f == 0:
            acc[...] = term
        else:
            acc[...] += term
    db_copy.wait()
    values = db_buf[...].astype(F32).reshape(rows * span, width)
    scaling = lax.rsqrt(jnp.mean(values * values, axis=-1, keepdims=True) + EPSILON)
    unit = values * scaling
    grad_unit = acc[...] * gain_ref[...]
    mean = jnp.mean(grad_unit * unit, axis=-1, keepdims=True)
    result = grad_enc + scaling * (grad_unit - unit * mean)
    out_ref[...] = result.reshape(rows, span, width)


def encode_back_call(dims, shard_t, row_t, gain, db4, pre, w_in, w_out, chunks):
    n_seq, cap, nb_here, rows, span, width, hidden_n, tile = dims
    steps = hidden_n // tile
    return pl.pallas_call(
        lambda *refs: encode_back_kernel(dims, *refs),
        out_shape=jax.ShapeDtypeStruct((rows, span, width), F32),
        in_specs=[SMEM_SPEC] * 2 + [VMEM_SPEC] + [ANY_SPEC] * 4 + [VMEM_SPEC] * n_seq,
        out_specs=VMEM_SPEC,
        scratch_shapes=[
            pltpu.VMEM((rows, span, width), BF16),
            pltpu.VMEM((rows * span, hidden_n), F32),
            pltpu.VMEM((steps, width, tile), BF16),
            pltpu.VMEM((steps, tile, width), BF16),
            pltpu.VMEM((rows, span, width), F32),
            pltpu.VMEM((rows * span, width), F32),
            pltpu.SemaphoreType.DMA,
            pltpu.SemaphoreType.DMA,
            pltpu.SemaphoreType.DMA((steps, 2)),
        ],
        cost_estimate=cost(4 * rows * span * width * hidden_n, 4 * width * hidden_n),
        name="encode_back",
    )(shard_t, row_t, gain, db4, pre, w_in, w_out, *chunks)


def swap(array, axis, bit):
    count = lax.axis_size(axis)
    return lax.ppermute(array, axis, [(i, i ^ bit) for i in range(count)])


def fast_body(
    tokens,
    database,
    nb_shard,
    nb_row,
    dec_gain,
    enc_gain,
    w_in,
    w_out,
    w_query,
    w_key,
    w_value,
    w_proj,
    grad_out,
):
    n_seq, n_mp = lax.axis_size("seq"), lax.axis_size("mp")
    tok_rows = tokens.shape[0]
    nb_here = tok_rows // STRETCH * K
    cap = max(1, (nb_here + n_seq - 1) // n_seq)
    rows, length, width = database.shape
    span = length // n_mp
    hidden_n = w_in.shape[1]
    dims = (n_seq, cap, nb_here, rows, span, width, hidden_n, 256)
    shard_t, row_t = nb_shard.T, nb_row.T
    enc_row, dec_row = enc_gain[None, :], dec_gain[None, :]
    db4 = database.reshape(rows, n_mp, span, width)
    far_first = sorted(range(1, n_seq), reverse=True)

    *outgoing, pre_act = encode_call(dims, shard_t, row_t, enc_row, db4, w_in, w_out)
    own = [outgoing[0]] + [None] * (n_seq - 1)
    for k in far_first:
        own[k] = swap(outgoing[k], "seq", k)
    across = [None] * n_seq
    for k in [0] + far_first:
        across[k] = swap(own[k], "mp", 2)
    query = query_call(tokens, dec_row, w_query, 128)
    grad_ctx = grad_ctx_call(grad_out, w_proj, 128)
    packed = pack_call((n_seq, cap, nb_here), shard_t, row_t, own, across)
    mine = packed.reshape(2, nb_here * span, width)
    part = swap(mine, "mp", 1)

    stretches = tok_rows // STRETCH
    halves = 2
    count = stretches // halves
    contexts, grad_queries, terms = [], [], []
    for p in range(halves):
        context, grad_query, keep, send = attend_call(
            p * count, count, mine, part, query, grad_ctx, w_key, w_value
        )
        contexts.append(context)
        grad_queries.append(grad_query)
        recv = swap(send, "mp", 1)
        onward = (keep[1].astype(F32) + recv[1].astype(F32)).astype(BF16)
        shape = (2, count * K, span, width)
        terms += [
            keep.reshape(shape),
            recv.reshape(shape),
            swap(onward, "mp", 2).reshape(shape[1:]),
        ]
    spread = spread_call((n_seq, cap, nb_here, halves), shard_t, row_t, terms)
    back = [spread[0]] + [None] * (n_seq - 1)
    for k in far_first:
        back[k] = swap(spread[k], "seq", k)

    def finish(keep, send):
        recv = swap(send, "mp", 1)
        onward = (keep[1].astype(F32) + recv[1].astype(F32)).astype(BF16)
        far = swap(onward, "mp", 2)
        return keep[0].astype(F32) + recv[0].astype(F32) + far.astype(F32)

    cca = finish(*project_call(jnp.concatenate(contexts), w_proj, 128)).astype(BF16)
    grad_tokens = finish(
        *tok_grad_call(tokens, dec_row, jnp.concatenate(grad_queries), w_query, 128)
    )
    grad_database = encode_back_call(
        dims, shard_t, row_t, enc_row, db4, pre_act, w_in, w_out, back
    )
    return (cca, grad_tokens, grad_database)


def solution(mesh):
    in_specs = (
        P("seq", None),
        P("seq", None, None),
        P(),
        P(),
        P(),
        P(),
        P(),
        P(),
        P(None, "mp"),
        P(None, "mp"),
        P(None, "mp"),
        P("mp", None),
        P("seq", None),
    )
    out_specs = (P("seq", "mp"), P("seq", "mp"), P("seq", "mp", None))
    body = fast_body if fast_ok(mesh) else general_body
    return jax.shard_map(body, mesh=mesh, in_specs=in_specs, out_specs=out_specs, check_vma=False)
```
